32 devices in a mesh: vol: 8 (over z, x), mem: 4 (over y, core).
Axes of the slice: x: 2, y: 2, z: 4, core: 2. Of those that a mesh axis runs over, the one named last changes fastest.
Arguments:
- potential: float32 [32, 256, 1024], P('vol', 'mem'), may hold values from -6 to 6
- conductivity: float32 [32, 256, 1024], P('vol', 'mem'), may hold values from 0.1 to 4
- ion_states: float32 [40, 524288], P(None, ('vol', 'mem')), may hold values from 0 to 1
- rate_scale: float32 [2, 40], replicated, may hold values from 0.05 to 2
- rate_slope: float32 [2, 40], replicated, may hold values from -1 to 1
- type_cond: float32 [3, 40], replicated, may hold values from 0.005 to 0.05
- reversal: float32 [40], replicated, may hold values from -2 to 2
- facet_counts: int32 [2048], P(('vol', 'mem')), may hold values from 0 to 256, as said below
- intra_voxel: int32 [524288], P(('vol', 'mem')), may hold values from 0 to 262143, as said below
- extra_voxel: int32 [524288], P(('vol', 'mem')), may hold values from 0 to 262143, as said below
- cell_type: int32 [2048], P(('vol', 'mem')), may hold values from 0 to 2
- gap_partner: int32 [2048, 8], P(('vol', 'mem')), may hold values from 0 to 2047, as said below
- gap_cond: float32 [2048, 8], P(('vol', 'mem')), may hold values from 0.2 to 2
Outputs:
- potential_next: float32 [32, 256, 1024], P('vol', 'mem')
- states_next: float32 [40, 524288], P(None, ('vol', 'mem'))
- membrane_current: float32 [524288], P(('vol', 'mem'))
The draws below stay inside these ranges and needn't reach their ends.
Inputs may be any that keep to these rules, and one draw needn't show every extreme that they name: `facet_counts`: within each brick's 64 cell slots, the cells with a positive count come first; a used cell has 64 to 256 facets; some brick has all its cells used and some cell uses all 256 slots. `intra_voxel`: local index x * 64 * 1024 + y * 1024 + z within the brick that holds the facet; the facets of the cell in slot s of its brick lie in local indices s * R to s * R + R - 1, with R = 4096. `extra_voxel`: local index x * 64 * 1024 + y * 1024 + z within the brick that holds the facet; the facets of the cell in slot s of its brick lie in local indices s * R to s * R + R - 1, with R = 4096. `gap_partner`: each partner is a cell with a positive count, in a brick whose first brick index differs from its own cell's by at most one.
All inputs are finite; a program needn't handle non-finite values.
Results may differ from the reference program's by a relative error of at most 0.0003.
Values sent between devices are 32-bit elements; how exact they have to be, the bound alone decides.
A program may use at most 64 MiB of HBM per device.

```python
import math
import jax
import jax.numpy as jnp
from jax import lax

CX = 4
CY = 64
CZ = 1024
CELL_DEV = 64
FPC = 256
NSTATES = 40
NTYPES = 3
JPC = 8
ITERS = 4
BRICKS_X = 8
BRICKS_Y = 4
NX = 32
NY = 256
NZ = 1024
CELLS = 2048
FACETS = 524288


def used_cells(key):
    first, second = jax.random.split(jax.random.fold_in(key, 11))
    bricks = BRICKS_X * BRICKS_Y
    occupied = jax.random.randint(first, (bricks,), max(1, CELL_DEV // 4), CELL_DEV + 1)
    fullest = jax.random.randint(second, (), 0, bricks)
    occupied = occupied.at[fullest].set(CELL_DEV)
    return (occupied.astype(jnp.int32), fullest)


def draw_facet_counts(key, part):
    occupied, fullest = used_cells(key)
    counts = jax.random.randint(jax.random.fold_in(key, 23), (CELLS,), max(1, FPC // 4), FPC + 1)
    cells = jnp.arange(CELLS, dtype=jnp.int32)
    counts = jnp.where(cells % CELL_DEV < occupied[cells // CELL_DEV], counts, 0)
    counts = counts.at[fullest * CELL_DEV].set(FPC)
    return counts.astype(jnp.int32)


def facet_voxels(key, salt):
    region = CX * CY * CZ // CELL_DEV
    facets = jnp.arange(FACETS, dtype=jnp.int32)
    slot = facets // FPC % CELL_DEV
    inner = jax.random.randint(jax.random.fold_in(key, salt), (FACETS,), 0, region)
    local = slot * region + inner
    local = local.at[0].set(0)
    local = local.at[FACETS - 1].set(CX * CY * CZ - 1)
    return local.astype(jnp.int32)


def draw_intra_voxel(key, part):
    return facet_voxels(key, 51)


def draw_extra_voxel(key, part):
    return facet_voxels(key, 53)


def draw_gap_partner(key, part):
    occupied, fullest = used_cells(key)
    keys = jax.random.split(jax.random.fold_in(key, 37), 3)
    cells = jnp.arange(CELLS, dtype=jnp.int32)
    brick_x = cells // CELL_DEV // BRICKS_Y
    offset = jax.random.randint(keys[0], (CELLS, JPC), -1, 2)
    other_x = jnp.clip(brick_x[:, None] + offset, 0, BRICKS_X - 1)
    other_y = jax.random.randint(keys[1], (CELLS, JPC), 0, BRICKS_Y)
    other_brick = other_x * BRICKS_Y + other_y
    other_slot = jax.random.randint(keys[2], (CELLS, JPC), 0, 1 << 20) % occupied[other_brick]
    return (other_brick * CELL_DEV + other_slot).astype(jnp.int32)


def plant(drawn, stream_key, smallest, high):
    longest = drawn.shape.index(max(drawn.shape))
    spots = []
    for shift in (0, 1):
        where = [jax.random.randint(jax.random.fold_in(stream_key, axis), (), 0, length) for axis, length in enumerate(drawn.shape)]
        where[longest] = (where[longest] + shift) % drawn.shape[longest]
        spots.append(tuple(where))
    return drawn.at[spots[0]].set(smallest).at[spots[1]].set(high)


def steps_of(stream_key, shape, cuts, low, high):
    def one(dim, shards_of):
        heights = jax.random.uniform(jax.random.fold_in(jax.random.fold_in(stream_key, 6), dim), (shards_of,), jnp.float32, low / len(cuts), high / len(cuts))
        return jnp.repeat(jnp.exp(heights), shape[dim] // shards_of).reshape((-1,) + (1,) * (len(shape) - dim - 1))

    factor_of = one(*cuts[0])
    for cut in cuts[1:]:
        factor_of = factor_of * one(*cut)
    return factor_of


def bell_draw(own_key, extent, scale, limit, cuts=(), kind=jnp.bfloat16):
    loudness = steps_of(own_key, extent, cuts, -0.22, 0.18) if cuts else 1.0
    entries = jax.random.normal(own_key, extent, jnp.float32) * scale * loudness
    return jnp.minimum(jnp.maximum(entries, -limit), limit).astype(kind)


def setup_inputs(seed: int = 0) -> dict:
    key_list = jax.random.split(jax.random.key(seed), 14)
    return {
        "potential": bell_draw(key_list[0], (NX, NY, NZ), 1.0, 6.0, ((0, 8), (1, 4)), jnp.float32),
        "conductivity": jnp.clip(jnp.exp(math.log(4.0) - 3.6888794 * jax.random.uniform(key_list[1], (NX, NY, NZ), jnp.float32) ** steps_of(key_list[1], (NX, NY, NZ), ((0, 8), (1, 4)), -0.2, 0.2)), 0.1, 4.0),
        "ion_states": jnp.clip(1.0 * jax.random.uniform(key_list[2], (NSTATES, FACETS), jnp.float32) ** steps_of(key_list[2], (NSTATES, FACETS), ((1, 32),), -0.2, 0.2), 0.0, 1.0),
        "rate_scale": jnp.clip(jnp.exp(jax.random.uniform(key_list[3], (2, NSTATES), jnp.float32, math.log(0.05), math.log(2.0))), 0.05, 2.0),
        "rate_slope": jnp.clip(jax.random.uniform(key_list[4], (2, NSTATES), jnp.float32, -1.0, 1.0), -1.0, 1.0),
        "type_cond": jnp.clip(jnp.exp(jax.random.uniform(key_list[5], (NTYPES, NSTATES), jnp.float32, math.log(0.005), math.log(0.05))), 0.005, 0.05),
        "reversal": jnp.clip(jax.random.uniform(key_list[6], (NSTATES,), jnp.float32, -2.0, 2.0), -2.0, 2.0),
        "facet_counts": draw_facet_counts(jax.random.fold_in(key_list[13], 71), 0),
        "intra_voxel": draw_intra_voxel(jax.random.fold_in(key_list[13], 71), 0),
        "extra_voxel": draw_extra_voxel(jax.random.fold_in(key_list[13], 71), 0),
        "cell_type": plant(jax.random.randint(key_list[10], (CELLS,), 0, NTYPES), jax.random.fold_in(key_list[10], 1), 0, NTYPES - 1).astype(jnp.int32),
        "gap_partner": draw_gap_partner(jax.random.fold_in(key_list[13], 71), 0),
        "gap_cond": jnp.clip(jnp.exp(math.log(2.0) - 2.3025851 * jax.random.uniform(key_list[12], (CELLS, JPC), jnp.float32) ** steps_of(key_list[12], (CELLS, JPC), ((0, 32),), -0.2, 0.2)), 0.2, 2.0),
    }


mass_coef = 1.0
time_step = 0.5
low_eig = 0.2
high_eig = 1.8


def neighbour_views(extended):
    padded = jnp.pad(extended, ((0, 0), (0, 0), (1, 1)))
    centre = padded[1:-1, 1:-1, 1:-1]
    views = (padded[:-2, 1:-1, 1:-1], padded[2:, 1:-1, 1:-1], padded[1:-1, :-2, 1:-1],
             padded[1:-1, 2:, 1:-1], padded[1:-1, 1:-1, :-2], padded[1:-1, 1:-1, 2:])
    return centre, views


def face_coeffs(cond_ext):
    centre, views = neighbour_views(cond_ext)
    coeffs = tuple(0.5 * (centre + other) for other in views)
    diagonal = mass_coef + time_step * (coeffs[0] + coeffs[1] + coeffs[2] + coeffs[3] + coeffs[4] + coeffs[5])
    return coeffs, diagonal


def operator_apply(field_ext, coeffs, diagonal):
    centre, views = neighbour_views(field_ext)
    total = coeffs[0] * views[0]
    for number in range(1, 6):
        total = total + coeffs[number] * views[number]
    return diagonal * centre - time_step * total


def chebyshev(apply_fn, rhs_field, start, diagonal, inside):
    theta = 0.5 * (high_eig + low_eig)
    delta = 0.5 * (high_eig - low_eig)
    sigma_one = theta / delta
    cheb_rho = 1.0 / sigma_one
    iterate = start
    resid = inside * (rhs_field - apply_fn(iterate)) / diagonal
    update = resid / theta
    for sweep in range(ITERS):
        iterate = iterate + update
        if sweep + 1 < ITERS:
            resid = inside * (rhs_field - apply_fn(iterate)) / diagonal
            rho_next = 1.0 / (2.0 * sigma_one - cheb_rho)
            update = rho_next * cheb_rho * update + (2.0 * rho_next / delta) * resid
            cheb_rho = rho_next
    return iterate


def ionic_update(states, voltage, type_flat, rate_scale, rate_slope, type_cond, reversal):
    opening = rate_scale[0][:, None] * jnp.exp(rate_slope[0][:, None] * voltage[None, :])
    closing = rate_scale[1][:, None] * jnp.exp(-rate_slope[1][:, None] * voltage[None, :])
    total = opening + closing
    steady = opening / total
    fresh = steady + (states - steady) * jnp.exp(-time_step * total)
    weighted = jnp.dot(type_cond, fresh, precision=lax.Precision.HIGHEST)
    offsets = jnp.dot(type_cond * reversal[None, :], fresh, precision=lax.Precision.HIGHEST)
    kinds = jnp.arange(type_cond.shape[0], dtype=jnp.int32)
    onehot = (type_flat[None, :] == kinds[:, None]).astype(fresh.dtype)
    ion_current = jnp.sum(onehot * (weighted * voltage[None, :] - offsets), axis=0)
    return fresh, ion_current


def reference(potential, conductivity, ion_states, rate_scale, rate_slope, type_cond, reversal, facet_counts, intra_voxel, extra_voxel, cell_type, gap_partner, gap_cond):
    bricks = BRICKS_X * BRICKS_Y
    facets_dev = CELL_DEV * FPC
    positions = jnp.arange(FACETS, dtype=jnp.int32)
    owner = positions // facets_dev
    brick_x = owner // BRICKS_Y
    brick_y = owner % BRICKS_Y

    def to_global(local):
        loc_x = local // (CY * CZ)
        loc_y = (local // CZ) % CY
        loc_z = local % CZ
        return (((brick_x * CX + loc_x) * NY + brick_y * CY + loc_y) * NZ + loc_z).astype(jnp.int32)

    global_in = to_global(intra_voxel)
    global_ex = to_global(extra_voxel)
    flat_field = potential.reshape(-1)
    voltage = flat_field[global_in] - flat_field[global_ex]
    active = (jnp.arange(FPC, dtype=jnp.int32)[None, :] < facet_counts[:, None]).reshape(-1)
    divisor = jnp.maximum(facet_counts, 1).astype(potential.dtype)
    cell_volt = jnp.sum(jnp.where(active, voltage, 0.0).reshape(CELLS, FPC), axis=1) / divisor
    partner_volt = cell_volt[gap_partner]
    gap_current = jnp.sum(gap_cond * (cell_volt[:, None] - partner_volt), axis=1)
    gap_facet = jnp.repeat(gap_current / divisor, FPC)
    type_flat = jnp.repeat(cell_type, FPC)

    states_blocks = jnp.transpose(ion_states.reshape(NSTATES, bricks, facets_dev), (1, 0, 2))

    def per_block(items):
        return ionic_update(items[0], items[1], items[2], rate_scale, rate_slope, type_cond, reversal)

    fresh_blocks, current_blocks = lax.map(per_block, (states_blocks, voltage.reshape(bricks, facets_dev), type_flat.reshape(bricks, facets_dev)))
    fresh = jnp.transpose(fresh_blocks, (1, 0, 2)).reshape(NSTATES, FACETS)
    ion_current = current_blocks.reshape(FACETS)
    states_next = jnp.where(active[None, :], fresh, ion_states)
    membrane_current = jnp.where(active, ion_current + gap_facet, 0.0)

    source = jnp.zeros_like(flat_field).at[global_in].add(membrane_current).at[global_ex].add(-membrane_current)
    rhs_field = mass_coef * potential - time_step * source.reshape(potential.shape)

    def border(field):
        return jnp.pad(field, ((1, 1), (1, 1), (0, 0)))

    coeffs, diagonal = face_coeffs(border(conductivity))

    def apply_operator(field):
        return operator_apply(border(field), coeffs, diagonal)

    potential_next = chebyshev(apply_operator, rhs_field, potential, diagonal, 1.0)
    return potential_next, states_next, membrane_current
```

```python
import functools

import jax
import jax.numpy as jnp
from jax import lax
from jax.experimental import pallas as pl
from jax.experimental.pallas import tpu as pltpu
from jax.sharding import PartitionSpec as P

ITERS = 4
CHUNKS = 4

mass_coef = 1.0
time_step = 0.5
low_eig = 0.2
high_eig = 1.8

MESH = pl.DeviceIdType.MESH
F32 = jnp.float32
BF16 = jnp.bfloat16


def sweep_weights():
    theta = 0.5 * (high_eig + low_eig)
    delta = 0.5 * (high_eig - low_eig)
    sigma_one = theta / delta
    rho = 1.0 / sigma_one
    pairs = [(0.0, 1.0 / theta)]
    for _ in range(ITERS - 1):
        rho_next = 1.0 / (2.0 * sigma_one - rho)
        pairs.append((rho_next * rho, 2.0 * rho_next / delta))
        rho = rho_next
    return pairs


def split2(x):
    hi = x.astype(BF16)
    lo = (x - hi.astype(F32)).astype(BF16)
    return hi, lo


def kernel(
    n_vol, n_mem, ntypes,
    *refs,
):
    count = 13
    body(n_vol, n_mem, ntypes, refs[:count], *refs[count:])


def home(n_vol, n_mem, v, m):
    if n_vol % 2 or n_mem % 2:
        return v, m
    d = lax.rem(m, 2) - lax.rem(v, 2)
    return v + d, m - d


def body(
    n_vol, n_mem, ntypes, given,
    out_pot, out_states, out_cur,
    pot, states, rate_scale, rate_slope, type_cond, reversal, counts, kinds, partner, gcond,
    sl, IN, EX, CUR, EDGE,
    X, C, K, R, U, HX, YS, YR, PB, VOLT, CVS, CV,
    sx_send, sx_recv, sy_send, sy_recv, sc_send, sc_recv, sb_send, sb_recv, st_send, st_recv, sr_send, sr_recv,
):
    CX, CY, CZ = pot.shape
    nstates, facets = states.shape
    cells = counts.shape[0]
    fpc = facets // cells
    groups, _, gf = IN.shape[1:]
    gcells = gf // fpc
    ybs = CY // 8
    zts = CZ // 128
    crow = CY // CHUNKS
    g_pot, g_cond, g_states, g_rs, g_rl, g_tc, g_rev, g_cnt, g_kind, g_in, g_ex, g_part, g_gc = given
    pairs = (
        (g_pot, pot), (g_in, IN.at[0]), (g_ex, EX.at[0]), (g_cnt, counts), (g_kind, kinds),
        (g_cond.at[:, pl.ds(0, 8)], EDGE.at[0]), (g_cond.at[:, pl.ds(CY - 8, 8)], EDGE.at[1]),
        (g_rs, rate_scale), (g_rl, rate_slope), (g_tc, type_cond), (g_rev, reversal), (g_states, states),
        (g_part, partner), (g_gc, gcond),
    )
    loads = [pltpu.make_async_copy(src, dst, sl.at[i]) for i, (src, dst) in enumerate(pairs)]
    for load in loads:
        load.start()
    me_v = lax.axis_index("vol")
    me_m = lax.axis_index("mem")
    trades = n_vol % 2 == 0 and n_mem % 2 == 0
    role_v, role_m = home(n_vol, n_mem, me_v, me_m)
    away = role_v != me_v
    stays = role_v == me_v
    sel = away.astype(jnp.int32)
    own = ((me_v > 0, me_v < n_vol - 1), (me_m > 0, me_m < n_mem - 1))
    has = ((role_v > 0, role_v < n_vol - 1), (role_m > 0, role_m < n_mem - 1))

    def x_peer(side):
        return home(n_vol, n_mem, role_v + (1 if side else -1), role_m)

    def y_peer(e, side):
        if e < 2:
            return home(n_vol, n_mem, me_v, me_m + (1 if side else -1))
        return home(n_vol, n_mem, role_v, role_m + (1 if side else -1))

    def y_ok(e, side):
        return (own if e < 2 else has)[1][side]

    peers = []
    for dv in (-1, 0, 1):
        for dm in range(n_mem):
            if dv == 0 and dm == 0:
                continue
            other_m = lax.rem(me_m + dm, n_mem)
            ok = None if dv == 0 else own[0][0 if dv < 0 else 1]
            peers.append((dv, dm, other_m, ok))

    def guarded(ok, fn):
        if ok is None:
            fn()
        else:
            pl.when(ok)(fn)

    barrier = pltpu.get_barrier_semaphore()
    for dv, dm, other_m, ok in peers:
        def greet(dv=dv, other_m=other_m):
            pl.semaphore_signal(barrier, inc=1, device_id=(me_v + dv, other_m), device_id_type=MESH)
        guarded(ok, greet)
    columns = 1 + own[0][0].astype(jnp.int32) + own[0][1].astype(jnp.int32)
    expected = columns * n_mem - 1
    if trades:
        odd = lax.rem(me_m, 2)
        far_v, far_m = me_v + 4 * odd - 2, me_m + 1 - 2 * odd
        far_ok = jnp.logical_and(far_v >= 0, far_v < n_vol)

        @pl.when(far_ok)
        def _():
            pl.semaphore_signal(barrier, inc=1, device_id=(far_v, far_m), device_id_type=MESH)
        expected = expected + far_ok.astype(jnp.int32)
    pl.semaphore_wait(barrier, expected)

    order = [0] + ([CX - 1] if CX > 1 else []) + list(range(1, CX - 1))

    def bulk_refs(e, p):
        return (g_cond, g_pot)[e].at[p], (C if e == 0 else X.at[0]).at[p, pl.ds(8, CY)]

    def bulk_far(e, p):
        src, dst = bulk_refs(e, p)
        return pltpu.make_async_remote_copy(
            src_ref=src, dst_ref=dst, send_sem=sb_send.at[e, p], recv_sem=sb_recv.at[e, p],
            device_id=(role_v, role_m), device_id_type=MESH,
        )

    def bulk_near(e, p):
        src, dst = bulk_refs(e, p)
        return pltpu.make_async_copy(src, dst, sb_recv.at[e, p])

    def table_far(k):
        src, dst = ((g_in, IN.at[1]), (g_ex, EX.at[1]), (CUR.at[0], CUR.at[1]))[k]
        return pltpu.make_async_remote_copy(
            src_ref=src, dst_ref=dst, send_sem=st_send.at[k], recv_sem=st_recv.at[k],
            device_id=(role_v, role_m), device_id_type=MESH,
        )

    def back_far(p, ch):
        rows = pl.ds(ch * crow, crow)
        return pltpu.make_async_remote_copy(
            src_ref=X.at[0, p, pl.ds(8 + ch * crow, crow)], dst_ref=out_pot.at[p, rows],
            send_sem=sr_send.at[p, ch], recv_sem=sr_recv.at[p, ch],
            device_id=(role_v, role_m), device_id_type=MESH,
        )

    def back_near(p, ch):
        rows = pl.ds(ch * crow, crow)
        return pltpu.make_async_copy(
            X.at[0, p, pl.ds(8 + ch * crow, crow)], out_pot.at[p, rows], sr_recv.at[p, ch]
        )

    def either(far, near):
        if trades:
            pl.when(away)(far)
            pl.when(stays)(near)
        else:
            near()

    def bulk_start():
        edge, inner = order[:2], order[2:]

        def far():
            for e in (0, 1):
                for p in edge:
                    bulk_far(e, p).start()
            table_far(0).start()
            table_far(1).start()
            for e in (0, 1):
                for p in inner:
                    bulk_far(e, p).start()

        def near():
            for e in (0, 1):
                for p in order:
                    bulk_near(e, p).start()
        either(far, near)

    def bulk_wait(e, planes):
        def far():
            for p in planes:
                bulk_far(e, p).wait_recv()

        def near():
            for p in planes:
                bulk_near(e, p).wait()
        either(far, near)

    bulk_start()

    def x_copy(e, side, ch, plane_ref):
        rows = pl.ds(ch * crow, crow)
        return pltpu.make_async_remote_copy(
            src_ref=plane_ref,
            dst_ref=HX.at[e, 1 - side, rows],
            send_sem=sx_send.at[e, side, ch],
            recv_sem=sx_recv.at[e, 1 - side, ch],
            device_id=x_peer(side),
            device_id_type=MESH,
        )

    def y_copy(e, side):
        return pltpu.make_async_remote_copy(
            src_ref=YS.at[e, side],
            dst_ref=YR.at[e, 1 - side],
            send_sem=sy_send.at[e, side],
            recv_sem=sy_recv.at[e, 1 - side],
            device_id=y_peer(e, side),
            device_id_type=MESH,
        )

    def face_of(e, side, ch):
        plane = CX - 1 if side else 0
        src = C if e == 0 else X.at[e - 1]
        return src.at[plane, pl.ds(8 + ch * crow, crow)]

    def send_x(e, ch):
        for side in (0, 1):
            guarded(has[0][side], lambda side=side: x_copy(e, side, ch, face_of(e, side, ch)).start())

    def wait_x(e, ch):
        for side in (0, 1):
            def w(side=side):
                pltpu.make_async_remote_copy(
                    src_ref=HX.at[e, side, pl.ds(ch * crow, crow)],
                    dst_ref=HX.at[e, side, pl.ds(ch * crow, crow)],
                    send_sem=sx_send.at[e, side, ch],
                    recv_sem=sx_recv.at[e, side, ch],
                    device_id=x_peer(side),
                    device_id_type=MESH,
                ).wait_recv()
            guarded(has[0][side], w)

    def send_y(e):
        for side in (0, 1):
            guarded(y_ok(e, side), lambda side=side: y_copy(e, side).start())

    def wait_y(e):
        for side in (0, 1):
            def w(side=side):
                pltpu.make_async_remote_copy(
                    src_ref=YS.at[e, side],
                    dst_ref=YR.at[e, side],
                    send_sem=sy_send.at[e, side],
                    recv_sem=sy_recv.at[e, side],
                    device_id=y_peer(2, side),
                    device_id_type=MESH,
                ).wait_recv()
            guarded(has[1][side], w)

    for load in loads:
        load.wait()
    for e in (0, 1):
        for p in range(CX):
            if e == 0:
                YS[e, 0, p:p + 1, :] = EDGE[0, p, 0:1, :]
                YS[e, 1, p:p + 1, :] = EDGE[1, p, 7:8, :]
            else:
                YS[e, 0, p:p + 1, :] = pot[p, 0:1, :]
                YS[e, 1, p:p + 1, :] = pot[p, CY - 1:CY, :]
        send_y(e)

    for side in (0, 1):
        @pl.when(jnp.logical_not(has[0][side]))
        def _(side=side):
            def zero(i, c):
                for e in range(ITERS + 1):
                    HX[e, side, pl.ds(pl.multiple_of(i * 8, 8), 8), :] = jnp.zeros((8, CZ), F32)
                return c
            lax.fori_loop(0, ybs, zero, 0)

        @pl.when(jnp.logical_not(own[0][side]))
        def _(side=side):
            for dm in range(n_mem):
                CV[(2 if side else 0) * n_mem + dm] = jnp.zeros((8, 128), F32)

        @pl.when(jnp.logical_not(has[1][side]))
        def _(side=side):
            for e in range(ITERS + 1):
                YR[e, side] = jnp.zeros((8, CZ), F32)

    eye = lax.broadcasted_iota(jnp.int32, (nstates, nstates), 0) == lax.broadcasted_iota(
        jnp.int32, (nstates, nstates), 1
    )
    columns = [rate_scale[0:1, :], rate_slope[0:1, :], rate_scale[1:2, :], rate_slope[1:2, :]]
    columns += [reversal[...]] + [type_cond[k:k + 1, :] for k in range(ntypes)]
    for k, col in enumerate(columns):
        spread = jnp.where(eye, jnp.broadcast_to(col, (nstates, nstates)), 0.0)
        PB[k] = jnp.broadcast_to(jnp.sum(spread, axis=1, keepdims=True), (nstates, 128))

    lane1 = lax.broadcasted_iota(jnp.int32, (1, 128), 1)
    slot_k = lax.broadcasted_iota(jnp.int32, (1, fpc), 1)

    def gather(g, acc):
        gx, gy = g // ybs, g % ybs
        tile = pot[gx, pl.ds(pl.multiple_of(gy * 8, 8), 8), :]
        block = jnp.concatenate([tile[:, z * 128:(z + 1) * 128] for z in range(zts)], axis=0)
        hi, lo = split2(block)
        lhs = jnp.concatenate([hi, lo], axis=0)
        picked = []
        for i, ref in enumerate((IN, EX)):
            idx = ref[0, g]
            lane = idx & 127
            row = ((idx >> 7) & (zts - 1)) * 8 + ((idx // CZ) & 7)
            hot = lax.broadcasted_iota(jnp.int32, (128, gf), 0) == lane
            table = jnp.where(hot, 1.0, 0.0).astype(BF16)
            got = jnp.dot(lhs, table, preferred_element_type=F32)
            half = got.shape[0] // 2
            got = got[:half] + got[half:]
            mask = lax.broadcasted_iota(jnp.int32, (8 * zts, gf), 0) == row
            picked.append(jnp.sum(jnp.where(mask, got, 0.0), axis=0, keepdims=True))
        volt = picked[0] - picked[1]
        VOLT[g] = volt
        for q in range(gcells):
            c = g * gcells + q
            cnt = counts[c]
            part = jnp.where(slot_k < cnt, volt[:, q * fpc:(q + 1) * fpc], 0.0)
            total = jnp.sum(part, axis=1, keepdims=True)
            div = jnp.maximum(jnp.full((1, 128), cnt, jnp.int32), 1).astype(F32)
            acc = jnp.where(lane1 == c, total / div, acc)
        return acc

    cell_volt = lax.fori_loop(0, groups, gather, jnp.zeros((1, 128), F32))
    CVS[...] = jnp.broadcast_to(cell_volt, (8, 128))
    CV[n_mem + me_m] = jnp.broadcast_to(cell_volt, (8, 128))

    def cv_copy(dv, dm, other_m):
        return pltpu.make_async_remote_copy(
            src_ref=CVS,
            dst_ref=CV.at[(1 - dv) * n_mem + me_m],
            send_sem=sc_send.at[(dv + 1) * n_mem + dm],
            recv_sem=sc_recv.at[(1 - dv) * n_mem + me_m],
            device_id=(me_v + dv, other_m),
            device_id_type=MESH,
        )

    def cv_wait(dv, dm, other_m):
        pltpu.make_async_remote_copy(
            src_ref=CVS,
            dst_ref=CV.at[(1 + dv) * n_mem + other_m],
            send_sem=sc_send.at[(dv + 1) * n_mem + dm],
            recv_sem=sc_recv.at[(1 + dv) * n_mem + other_m],
            device_id=(me_v + dv, other_m),
            device_id_type=MESH,
        ).wait_recv()

    for dv, dm, other_m, ok in peers:
        guarded(ok, lambda a=dv, b=dm, o=other_m: cv_copy(a, b, o).start())

    def ionic(g, carry):
        for q in range(gcells):
            c = g * gcells + q
            cnt = counts[c]
            kind = jnp.full((nstates, 128), kinds[c], jnp.int32)
            tc = PB[5]
            for k in range(1, ntypes):
                tc = jnp.where(kind == k, PB[5 + k], tc)
            for h in range(fpc // 128):
                off = q * fpc + h * 128
                v = VOLT[g, :, off:off + 128]
                lanes = pl.ds(pl.multiple_of(g * gf + off, 128), 128)
                st = states[:, lanes]
                opening = PB[0] * jnp.exp(PB[1] * v)
                closing = PB[2] * jnp.exp(-(PB[3] * v))
                total = opening + closing
                steady = opening / total
                fresh = steady + (st - steady) * jnp.exp(-time_step * total)
                live = (lane1 + h * 128) < cnt
                out_states[:, lanes] = jnp.where(live, fresh, st)
                cur = jnp.sum(tc * fresh * (v - PB[4]), axis=0, keepdims=True)
                out_cur[g, :, off:off + 128] = cur
        return carry

    lax.fori_loop(0, groups, ionic, 0)

    for e in (0, 1):
        bulk_wait(e, order[:2])
        for ch in range(CHUNKS):
            send_x(e, ch)

    for dv, dm, other_m, ok in peers:
        guarded(ok, lambda a=dv, b=dm, o=other_m: cv_wait(a, b, o))

    nb = 3 * n_mem
    band = jnp.concatenate([CV[i, 0:1, :] for i in range(nb)] + [jnp.zeros((-nb % 16, 128), F32)], axis=0)
    hi, mid = split2(band)
    rest = (band - hi.astype(F32) - mid.astype(F32)).astype(BF16)
    lhs = jnp.concatenate([hi, mid, rest], axis=0)
    nbr = nb + (-nb % 16)
    gap = jnp.zeros((1, cells), F32)
    for j in range(partner.shape[0]):
        pos = partner[j:j + 1, :]
        slot_row = pos // cells - (me_v - 1) * n_mem
        col = pos % cells
        table = jnp.where(lax.broadcasted_iota(jnp.int32, (128, cells), 0) == col, 1.0, 0.0).astype(BF16)
        got = jnp.dot(lhs, table, preferred_element_type=F32)
        got = got[:nbr] + got[nbr:2 * nbr] + got[2 * nbr:]
        mask = lax.broadcasted_iota(jnp.int32, (nbr, cells), 0) == slot_row
        pv = jnp.sum(jnp.where(mask, got, 0.0), axis=0, keepdims=True)
        gap = gap + gcond[j:j + 1, :] * (cell_volt[:, :cells] - pv)

    def finish(g, carry):
        cur = []
        for q in range(gcells):
            c = g * gcells + q
            cnt = counts[c]
            share = jnp.sum(jnp.where(lane1[:, :cells] == c, gap, 0.0), axis=1, keepdims=True)
            share = share / jnp.maximum(jnp.full((1, fpc), cnt, jnp.int32), 1).astype(F32)
            ion = out_cur[g, :, q * fpc:(q + 1) * fpc]
            cur.append(jnp.where(slot_k < cnt, ion + share, 0.0))
        cur = jnp.concatenate(cur, axis=1)
        out_cur[g] = cur
        CUR[0, g] = cur
        return carry

    lax.fori_loop(0, groups, finish, 0)
    if trades:
        @pl.when(away)
        def _():
            table_far(2).start()
            for k in range(3):
                table_far(k).wait_recv()

    def scatter(g, carry):
        cur = CUR[sel, g]
        hi = cur.astype(BF16).astype(F32)
        lo = cur - hi
        source = None
        for i, ref in enumerate((IN, EX)):
            idx = ref[sel, g]
            lane = idx & 127
            hot = lax.broadcasted_iota(jnp.int32, (128, gf), 0) == lane
            table = jnp.where(hot, 1.0, 0.0).astype(BF16)
            row = ((idx >> 7) & (zts - 1)) * 8 + ((idx // CZ) & 7)
            mask = lax.broadcasted_iota(jnp.int32, (8 * zts, gf), 0) == row
            sign = 1.0 if i == 0 else -1.0
            vals = jnp.concatenate(
                [jnp.where(mask, sign * part, 0.0).astype(BF16) for part in (hi, lo)], axis=0
            )
            put = lax.dot_general(vals, table, (((1,), (1,)), ((), ())), preferred_element_type=F32)
            source = put if source is None else source + put
        half = source.shape[0] // 2
        source = source[:half] + source[half:]
        gx, gy = g // ybs, g % ybs
        rows = pl.ds(pl.multiple_of(gy * 8, 8), 8)
        for z in range(zts):
            R[gx, rows, z * 128:(z + 1) * 128] = source[z * 8:(z + 1) * 8, :]
        return carry

    lax.fori_loop(0, groups, scatter, 0)

    for e in (0, 1):
        bulk_wait(e, order[2:])

    def put_y(dst, e):
        for p in range(CX):
            dst[p, 7:8, :] = YR[e, 0, p:p + 1, :]
            dst[p, 8 + CY:9 + CY, :] = YR[e, 1, p:p + 1, :]

    wait_y(0)
    put_y(C, 0)
    for ch in range(CHUNKS):
        wait_x(0, ch)
    lane = lax.broadcasted_iota(jnp.int32, (8, CZ), 1)
    sub = lax.broadcasted_iota(jnp.int32, (8, CZ), 0)

    def views(src, halo, p, yb):
        base = pl.multiple_of(yb * 8, 8)
        rows = pl.ds(base + 8, 8)
        own = pl.ds(base, 8)
        centre = src[p, rows, :]
        below = halo[0, own, :] if p == 0 else src[p - 1, rows, :]
        above = halo[1, own, :] if p == CX - 1 else src[p + 1, rows, :]
        before = src[p, pl.ds(base, 8), :]
        after = src[p, pl.ds(pl.multiple_of(base + 16, 8), 8), :]
        return own, centre, (
            below, above,
            pltpu.roll(jnp.where(sub == 7, before, centre), 1, 0),
            pltpu.roll(jnp.where(sub == 0, after, centre), 7, 0),
            pltpu.roll(centre, 1, 1), pltpu.roll(centre, CZ - 1, 1),
        )

    def coeffs(yb, carry):
        for p in range(CX):
            own, centre, near = views(C, HX.at[0], p, yb)
            near = list(near)
            near[4] = jnp.where(lane == 0, 0.0, near[4])
            near[5] = jnp.where(lane == CZ - 1, 0.0, near[5])
            faces = [centre + n for n in near]
            total = faces[0] + faces[1] + faces[2] + faces[3] + faces[4] + faces[5]
            inv = 1.0 / (mass_coef + (0.5 * time_step) * total)
            scale = (0.5 * time_step) * inv
            faces[4] = jnp.where(lane == 0, 0.0, faces[4])
            faces[5] = jnp.where(lane == CZ - 1, 0.0, faces[5])
            for k in range(6):
                K[k, p, own, :] = faces[k] * scale
            R[p, own, :] = (mass_coef * X[0, p, pl.ds(pl.multiple_of(yb * 8, 8) + 8, 8), :] - time_step * R[p, own, :]) * inv
        return carry

    lax.fori_loop(0, ybs, coeffs, 0)

    def back_start(planes, ch):
        def far():
            for p in planes:
                back_far(p, ch).start()

        def near():
            for p in planes:
                back_near(p, ch).start()
        either(far, near)

    weights = sweep_weights()
    for t in range(ITERS):
        e = t + 1
        last = t == ITERS - 1
        wa, wb = weights[t]
        if last:
            for side in (0, 1):
                for ch in range(CHUNKS):
                    guarded(has[0][side], lambda s=side, ch=ch: x_copy(1, s, ch, face_of(1, s, ch)).wait_send())
        wait_y(e)
        put_y(X.at[t], e)

        def tile(p, yb, t=t, e=e, last=last, wa=wa, wb=wb):
            own, centre, near = views(X.at[t], HX.at[e], p, yb)
            acc = R[p, own, :] - centre
            for k in range(6):
                acc = acc + K[k, p, own, :] * near[k]
            step = wb * acc
            if t > 0:
                step = step + wa * U[p, own, :]
            new = centre + step
            if not last:
                U[p, own, :] = step
            X[(t + 1) % ITERS, p, pl.ds(pl.multiple_of(yb * 8, 8) + 8, 8), :] = new

        def inner(yb, carry, tile=tile):
            for p in range(1, CX - 1):
                tile(p, yb)
            return carry

        per = ybs // CHUNKS
        if last:
            for ch in range(CHUNKS):
                lax.fori_loop(ch * per, (ch + 1) * per, inner, 0)
                back_start(range(1, CX - 1), ch)
        else:
            lax.fori_loop(0, ybs, inner, 0)
        for ch in range(CHUNKS):
            wait_x(e, ch)

            def outer(yb, carry, tile=tile):
                tile(0, yb)
                if CX > 1:
                    tile(CX - 1, yb)
                return carry

            lax.fori_loop(ch * per, (ch + 1) * per, outer, 0)
            if last:
                back_start(order[:2], ch)
            else:
                send_x(e + 1, ch)
        if not last:
            for p in range(CX):
                YS[e + 1, 0, p:p + 1, :] = X[t + 1, p, 8:9, :]
                YS[e + 1, 1, p:p + 1, :] = X[t + 1, p, 7 + CY:8 + CY, :]
            send_y(e + 1)

    for e in range(ITERS + 1):
        for side in (0, 1):
            for ch in range(CHUNKS if e != 1 else 0):
                guarded(has[0][side], lambda e=e, s=side, ch=ch: x_copy(e, s, ch, face_of(e, s, ch)).wait_send())
            guarded(y_ok(e, side), lambda e=e, s=side: y_copy(e, s).wait_send())
    for dv, dm, other_m, ok in peers:
        guarded(ok, lambda a=dv, b=dm, o=other_m: cv_copy(a, b, o).wait_send())

    def drain_far():
        for e in (0, 1):
            for p in range(CX):
                bulk_far(e, p).wait_send()
        for k in range(3):
            table_far(k).wait_send()
        for p in range(CX):
            for ch in range(CHUNKS):
                back_far(p, ch).wait()

    def drain_near():
        for p in range(CX):
            for ch in range(CHUNKS):
                back_near(p, ch).wait()
    either(drain_far, drain_near)


def per_device(
    n_vol, n_mem,
    potential, conductivity, ion_states, rate_scale, rate_slope, type_cond, reversal,
    facet_counts, intra_voxel, extra_voxel, cell_type, gap_partner, gap_cond,
):
    CX, CY, CZ = potential.shape
    nstates, facets = ion_states.shape
    cells = facet_counts.shape[0]
    ntypes = type_cond.shape[0]
    groups = CX * CY // 8
    gf = facets // groups
    ncols = 5 + ntypes
    vmem = pl.BlockSpec(memory_space=pltpu.VMEM)
    ex = ITERS + 1
    nb = 3 * n_mem
    args = (
        potential, conductivity, ion_states, rate_scale, rate_slope, type_cond, reversal[None, :],
        facet_counts, cell_type,
        intra_voxel.reshape(groups, 1, gf), extra_voxel.reshape(groups, 1, gf), gap_partner.T, gap_cond.T,
    )
    args = tuple(pltpu.with_memory_space_constraint(a, pltpu.HBM) for a in args)
    held = [
        (pltpu.SMEM if a.ndim == 1 else pltpu.VMEM)(a.shape, a.dtype)
        for i, a in enumerate(args) if i not in (1, 9, 10)
    ]
    out = pl.pallas_call(
        functools.partial(kernel, n_vol, n_mem, ntypes),
        out_shape=(
            jax.ShapeDtypeStruct(potential.shape, F32),
            jax.ShapeDtypeStruct(ion_states.shape, F32),
            jax.ShapeDtypeStruct((groups, 1, gf), F32),
        ),
        in_specs=[pl.BlockSpec(memory_space=pltpu.HBM)] * len(args),
        out_specs=(vmem, vmem, vmem),
        scratch_shapes=held + [
            pltpu.SemaphoreType.DMA((14,)),
            pltpu.VMEM((2, groups, 1, gf), jnp.int32),
            pltpu.VMEM((2, groups, 1, gf), jnp.int32),
            pltpu.VMEM((2, groups, 1, gf), F32),
            pltpu.VMEM((2, CX, 8, CZ), F32),
            pltpu.VMEM((ITERS, CX, CY + 16, CZ), F32),
            pltpu.VMEM((CX, CY + 16, CZ), F32),
            pltpu.VMEM((6, CX, CY, CZ), F32),
            pltpu.VMEM((CX, CY, CZ), F32),
            pltpu.VMEM((CX, CY, CZ), F32),
            pltpu.VMEM((ex, 2, CY, CZ), F32),
            pltpu.VMEM((ex, 2, 8, CZ), F32),
            pltpu.VMEM((ex, 2, 8, CZ), F32),
            pltpu.VMEM((ncols, nstates, 128), F32),
            pltpu.VMEM((groups, 1, gf), F32),
            pltpu.VMEM((8, 128), F32),
            pltpu.VMEM((nb, 8, 128), F32),
            pltpu.SemaphoreType.DMA((ex, 2, CHUNKS)),
            pltpu.SemaphoreType.DMA((ex, 2, CHUNKS)),
            pltpu.SemaphoreType.DMA((ex, 2)),
            pltpu.SemaphoreType.DMA((ex, 2)),
            pltpu.SemaphoreType.DMA((nb,)),
            pltpu.SemaphoreType.DMA((nb,)),
            pltpu.SemaphoreType.DMA((2, CX)),
            pltpu.SemaphoreType.DMA((2, CX)),
            pltpu.SemaphoreType.DMA((3,)),
            pltpu.SemaphoreType.DMA((3,)),
            pltpu.SemaphoreType.DMA((CX, CHUNKS)),
            pltpu.SemaphoreType.DMA((CX, CHUNKS)),
        ],
        compiler_params=pltpu.CompilerParams(
            collective_id=0, has_side_effects=True, vmem_limit_bytes=42 * 1024 * 1024
        ),
    )(*args)
    return out[0], out[1], out[2].reshape(-1)


def solution(mesh):
    sizes = dict(mesh.shape)
    in_specs = (
        P("vol", "mem", None),
        P("vol", "mem", None),
        P(None, ("vol", "mem")),
        P(),
        P(),
        P(),
        P(),
        P(("vol", "mem")),
        P(("vol", "mem")),
        P(("vol", "mem")),
        P(("vol", "mem")),
        P(("vol", "mem"), None),
        P(("vol", "mem"), None),
    )
    out_specs = (P("vol", "mem", None), P(None, ("vol", "mem")), P(("vol", "mem")))
    return jax.shard_map(
        functools.partial(per_device, sizes["vol"], sizes["mem"]),
        mesh=mesh, in_specs=in_specs, out_specs=out_specs, check_vma=False,
    )
```

```python
import functools

import jax
import jax.numpy as jnp
from jax import lax
from jax.experimental import pallas as pl
from jax.experimental.pallas import tpu as pltpu
from jax.sharding import PartitionSpec as P

ITERS = 4
PARTS = 3

mass_coef = 1.0
time_step = 0.5
low_eig = 0.2
high_eig = 1.8

MESH = pl.DeviceIdType.MESH
F32 = jnp.float32
BF16 = jnp.bfloat16


def sweep_weights():
    theta = 0.5 * (high_eig + low_eig)
    delta = 0.5 * (high_eig - low_eig)
    sigma_one = theta / delta
    rho = 1.0 / sigma_one
    pairs = [(0.0, 1.0 / theta)]
    for _ in range(ITERS - 1):
        rho_next = 1.0 / (2.0 * sigma_one - rho)
        pairs.append((rho_next * rho, 2.0 * rho_next / delta))
        rho = rho_next
    return pairs


def row_spans(rows):
    if rows == 8:
        return [(0, 8)]
    blocks = rows // 8 - 2
    parts = max(1, min(PARTS, blocks))
    cuts = [8 + 8 * (blocks * i // parts) for i in range(parts + 1)]
    return [(0, 8), (rows - 8, 8)] + [(a, b - a) for a, b in zip(cuts, cuts[1:]) if b > a]


def split2(x):
    hi = x.astype(BF16)
    lo = (x - hi.astype(F32)).astype(BF16)
    return hi, lo


def kernel(
    n_vol, n_mem, ntypes,
    *refs,
):
    count = 13
    body(n_vol, n_mem, ntypes, refs[:count], *refs[count:])


def home(n_vol, n_mem, v, m):
    if n_vol % 2 or n_mem % 2:
        return v, m
    d = lax.rem(m, 2) - lax.rem(v, 2)
    return v + d, m - d


def body(
    n_vol, n_mem, ntypes, given,
    out_pot, out_states, out_cur,
    pot, states, rate_scale, rate_slope, type_cond, reversal, counts, kinds, partner, gcond,
    sl, IN, EX, CUR, EDGE,
    X, C, K, R, U, HX, YS, YR, PB, VOLT, CVS, CV,
    sx_send, sx_recv, sy_send, sy_recv, sc_send, sc_recv, sb_send, sb_recv, st_send, st_recv, sr_send, sr_recv,
):
    CX, CY, CZ = pot.shape
    nstates, facets = states.shape
    cells = counts.shape[0]
    fpc = facets // cells
    groups, _, gf = IN.shape[1:]
    gcells = gf // fpc
    ybs = CY // 8
    zts = CZ // 128
    spans = row_spans(CY)
    edges = 1 if ybs == 1 else 2
    g_pot, g_cond, g_states, g_rs, g_rl, g_tc, g_rev, g_cnt, g_kind, g_in, g_ex, g_part, g_gc = given
    pairs = (
        (g_pot, pot), (g_in, IN.at[0]), (g_ex, EX.at[0]), (g_cnt, counts), (g_kind, kinds),
        (g_cond.at[:, pl.ds(0, 8)], EDGE.at[0]), (g_cond.at[:, pl.ds(CY - 8, 8)], EDGE.at[1]),
        (g_rs, rate_scale), (g_rl, rate_slope), (g_tc, type_cond), (g_rev, reversal), (g_states, states),
        (g_part, partner), (g_gc, gcond),
    )
    loads = [pltpu.make_async_copy(src, dst, sl.at[i]) for i, (src, dst) in enumerate(pairs)]
    for load in loads:
        load.start()
    me_v = lax.axis_index("vol")
    me_m = lax.axis_index("mem")
    trades = n_vol % 2 == 0 and n_mem % 2 == 0
    role_v, role_m = home(n_vol, n_mem, me_v, me_m)
    away = role_v != me_v
    stays = role_v == me_v
    sel = away.astype(jnp.int32)
    own = ((me_v > 0, me_v < n_vol - 1), (me_m > 0, me_m < n_mem - 1))
    has = ((role_v > 0, role_v < n_vol - 1), (role_m > 0, role_m < n_mem - 1))

    def x_peer(side):
        return home(n_vol, n_mem, role_v + (1 if side else -1), role_m)

    def y_peer(e, side):
        if e < 2:
            return home(n_vol, n_mem, me_v, me_m + (1 if side else -1))
        return home(n_vol, n_mem, role_v, role_m + (1 if side else -1))

    def y_ok(e, side):
        return (own if e < 2 else has)[1][side]

    peers = []
    for dv in (-1, 0, 1):
        for dm in range(n_mem):
            if dv == 0 and dm == 0:
                continue
            other_m = lax.rem(me_m + dm, n_mem)
            ok = None if dv == 0 else own[0][0 if dv < 0 else 1]
            peers.append((dv, dm, other_m, ok))

    def guarded(ok, fn):
        if ok is None:
            fn()
        else:
            pl.when(ok)(fn)

    barrier = pltpu.get_barrier_semaphore()
    for dv, dm, other_m, ok in peers:
        def greet(dv=dv, other_m=other_m):
            pl.semaphore_signal(barrier, inc=1, device_id=(me_v + dv, other_m), device_id_type=MESH)
        guarded(ok, greet)
    columns = 1 + own[0][0].astype(jnp.int32) + own[0][1].astype(jnp.int32)
    expected = columns * n_mem - 1
    if trades:
        odd = lax.rem(me_m, 2)
        far_v, far_m = me_v + 4 * odd - 2, me_m + 1 - 2 * odd
        far_ok = jnp.logical_and(far_v >= 0, far_v < n_vol)

        @pl.when(far_ok)
        def _():
            pl.semaphore_signal(barrier, inc=1, device_id=(far_v, far_m), device_id_type=MESH)
        expected = expected + far_ok.astype(jnp.int32)
    pl.semaphore_wait(barrier, expected)

    order = [0] + ([CX - 1] if CX > 1 else []) + list(range(1, CX - 1))

    def bulk_refs(e, p):
        return (g_cond, g_pot)[e].at[p], (C if e == 0 else X.at[0]).at[p, pl.ds(8, CY)]

    def bulk_far(e, p):
        src, dst = bulk_refs(e, p)
        return pltpu.make_async_remote_copy(
            src_ref=src, dst_ref=dst, send_sem=sb_send.at[e, p], recv_sem=sb_recv.at[e, p],
            device_id=(role_v, role_m), device_id_type=MESH,
        )

    def bulk_near(e, p):
        src, dst = bulk_refs(e, p)
        return pltpu.make_async_copy(src, dst, sb_recv.at[e, p])

    def table_far(k):
        src, dst = ((g_in, IN.at[1]), (g_ex, EX.at[1]), (CUR.at[0], CUR.at[1]))[k]
        return pltpu.make_async_remote_copy(
            src_ref=src, dst_ref=dst, send_sem=st_send.at[k], recv_sem=st_recv.at[k],
            device_id=(role_v, role_m), device_id_type=MESH,
        )

    def back_far(p, ch):
        start, size = spans[ch]
        rows = pl.ds(start, size)
        return pltpu.make_async_remote_copy(
            src_ref=X.at[0, p, pl.ds(8 + start, size)], dst_ref=out_pot.at[p, rows],
            send_sem=sr_send.at[p, ch], recv_sem=sr_recv.at[p, ch],
            device_id=(role_v, role_m), device_id_type=MESH,
        )

    def back_near(p, ch):
        start, size = spans[ch]
        rows = pl.ds(start, size)
        return pltpu.make_async_copy(
            X.at[0, p, pl.ds(8 + start, size)], out_pot.at[p, rows], sr_recv.at[p, ch]
        )

    def either(far, near):
        if trades:
            pl.when(away)(far)
            pl.when(stays)(near)
        else:
            near()

    def bulk_start(step):
        edge, inner = order[:2], order[2:]
        batch = ([(0, p) for p in edge], [(1, p) for p in edge], [(e, p) for e in (0, 1) for p in inner])[step]

        def far():
            for e, p in batch:
                bulk_far(e, p).start()
            if step == 0:
                table_far(0).start()
                table_far(1).start()

        def near():
            for e, p in batch:
                bulk_near(e, p).start()
        either(far, near)

    def bulk_wait(e, planes):
        def far():
            for p in planes:
                bulk_far(e, p).wait_recv()

        def near():
            for p in planes:
                bulk_near(e, p).wait()
        either(far, near)

    bulk_start(0)

    def x_copy(e, side, ch, plane_ref):
        rows = pl.ds(*spans[ch])
        return pltpu.make_async_remote_copy(
            src_ref=plane_ref,
            dst_ref=HX.at[e, 1 - side, rows],
            send_sem=sx_send.at[e, side, ch],
            recv_sem=sx_recv.at[e, 1 - side, ch],
            device_id=x_peer(side),
            device_id_type=MESH,
        )

    def y_copy(e, side):
        return pltpu.make_async_remote_copy(
            src_ref=YS.at[e, side],
            dst_ref=YR.at[e, 1 - side],
            send_sem=sy_send.at[e, side],
            recv_sem=sy_recv.at[e, 1 - side],
            device_id=y_peer(e, side),
            device_id_type=MESH,
        )

    def face_of(e, side, ch):
        plane = CX - 1 if side else 0
        src = C if e == 0 else X.at[e - 1]
        return src.at[plane, pl.ds(8 + spans[ch][0], spans[ch][1])]

    def send_x(e, ch):
        for side in (0, 1):
            guarded(has[0][side], lambda side=side: x_copy(e, side, ch, face_of(e, side, ch)).start())

    def wait_x(e, ch):
        for side in (0, 1):
            def w(side=side):
                pltpu.make_async_remote_copy(
                    src_ref=HX.at[e, side, pl.ds(*spans[ch])],
                    dst_ref=HX.at[e, side, pl.ds(*spans[ch])],
                    send_sem=sx_send.at[e, side, ch],
                    recv_sem=sx_recv.at[e, side, ch],
                    device_id=x_peer(side),
                    device_id_type=MESH,
                ).wait_recv()
            guarded(has[0][side], w)

    def send_y(e):
        for side in (0, 1):
            guarded(y_ok(e, side), lambda side=side: y_copy(e, side).start())

    def wait_y(e):
        for side in (0, 1):
            def w(side=side):
                pltpu.make_async_remote_copy(
                    src_ref=YS.at[e, side],
                    dst_ref=YR.at[e, side],
                    send_sem=sy_send.at[e, side],
                    recv_sem=sy_recv.at[e, side],
                    device_id=y_peer(2, side),
                    device_id_type=MESH,
                ).wait_recv()
            guarded(has[1][side], w)

    late = 11
    for i, load in enumerate(loads):
        if i != late:
            load.wait()
    for e in (0, 1):
        for p in range(CX):
            if e == 0:
                YS[e, 0, p:p + 1, :] = EDGE[0, p, 0:1, :]
                YS[e, 1, p:p + 1, :] = EDGE[1, p, 7:8, :]
            else:
                YS[e, 0, p:p + 1, :] = pot[p, 0:1, :]
                YS[e, 1, p:p + 1, :] = pot[p, CY - 1:CY, :]
        send_y(e)

    for side in (0, 1):
        @pl.when(jnp.logical_not(has[0][side]))
        def _(side=side):
            def zero(i, c):
                for e in range(ITERS + 1):
                    HX[e, side, pl.ds(pl.multiple_of(i * 8, 8), 8), :] = jnp.zeros((8, CZ), F32)
                return c
            lax.fori_loop(0, ybs, zero, 0)

        @pl.when(jnp.logical_not(own[0][side]))
        def _(side=side):
            for dm in range(n_mem):
                CV[(2 if side else 0) * n_mem + dm] = jnp.zeros((8, 128), F32)

        @pl.when(jnp.logical_not(has[1][side]))
        def _(side=side):
            for e in range(ITERS + 1):
                YR[e, side] = jnp.zeros((8, CZ), F32)

    eye = lax.broadcasted_iota(jnp.int32, (nstates, nstates), 0) == lax.broadcasted_iota(
        jnp.int32, (nstates, nstates), 1
    )
    columns = [rate_scale[0:1, :], rate_slope[0:1, :], rate_scale[1:2, :], rate_slope[1:2, :]]
    columns += [reversal[...]] + [type_cond[k:k + 1, :] for k in range(ntypes)]
    for k, col in enumerate(columns):
        spread = jnp.where(eye, jnp.broadcast_to(col, (nstates, nstates)), 0.0)
        PB[k] = jnp.broadcast_to(jnp.sum(spread, axis=1, keepdims=True), (nstates, 128))

    lane1 = lax.broadcasted_iota(jnp.int32, (1, 128), 1)
    slot_k = lax.broadcasted_iota(jnp.int32, (1, fpc), 1)

    def gather(g, acc):
        gx, gy = g // ybs, g % ybs
        tile = pot[gx, pl.ds(pl.multiple_of(gy * 8, 8), 8), :]
        block = jnp.concatenate([tile[:, z * 128:(z + 1) * 128] for z in range(zts)], axis=0)
        hi, lo = split2(block)
        lhs = jnp.concatenate([hi, lo], axis=0)
        picked = []
        for i, ref in enumerate((IN, EX)):
            idx = ref[0, g]
            lane = idx & 127
            row = ((idx >> 7) & (zts - 1)) * 8 + ((idx // CZ) & 7)
            hot = lax.broadcasted_iota(jnp.int32, (128, gf), 0) == lane
            table = jnp.where(hot, 1.0, 0.0).astype(BF16)
            got = jnp.dot(lhs, table, preferred_element_type=F32)
            half = got.shape[0] // 2
            got = got[:half] + got[half:]
            mask = lax.broadcasted_iota(jnp.int32, (8 * zts, gf), 0) == row
            picked.append(jnp.sum(jnp.where(mask, got, 0.0), axis=0, keepdims=True))
        volt = picked[0] - picked[1]
        VOLT[g] = volt
        for q in range(gcells):
            c = g * gcells + q
            cnt = counts[c]
            part = jnp.where(slot_k < cnt, volt[:, q * fpc:(q + 1) * fpc], 0.0)
            total = jnp.sum(part, axis=1, keepdims=True)
            div = jnp.maximum(jnp.full((1, 128), cnt, jnp.int32), 1).astype(F32)
            acc = jnp.where(lane1 == c, total / div, acc)
        return acc

    cell_volt = lax.fori_loop(0, groups, gather, jnp.zeros((1, 128), F32))
    CVS[...] = jnp.broadcast_to(cell_volt, (8, 128))
    CV[n_mem + me_m] = jnp.broadcast_to(cell_volt, (8, 128))

    def cv_copy(dv, dm, other_m):
        return pltpu.make_async_remote_copy(
            src_ref=CVS,
            dst_ref=CV.at[(1 - dv) * n_mem + me_m],
            send_sem=sc_send.at[(dv + 1) * n_mem + dm],
            recv_sem=sc_recv.at[(1 - dv) * n_mem + me_m],
            device_id=(me_v + dv, other_m),
            device_id_type=MESH,
        )

    def cv_wait(dv, dm, other_m):
        pltpu.make_async_remote_copy(
            src_ref=CVS,
            dst_ref=CV.at[(1 + dv) * n_mem + other_m],
            send_sem=sc_send.at[(dv + 1) * n_mem + dm],
            recv_sem=sc_recv.at[(1 + dv) * n_mem + other_m],
            device_id=(me_v + dv, other_m),
            device_id_type=MESH,
        ).wait_recv()

    for dv, dm, other_m, ok in peers:
        guarded(ok, lambda a=dv, b=dm, o=other_m: cv_copy(a, b, o).start())
    bulk_start(1)
    loads[late].wait()

    def ionic(g, carry):
        for q in range(gcells):
            c = g * gcells + q
            cnt = counts[c]
            kind = jnp.full((nstates, 128), kinds[c], jnp.int32)
            tc = PB[5]
            for k in range(1, ntypes):
                tc = jnp.where(kind == k, PB[5 + k], tc)
            for h in range(fpc // 128):
                off = q * fpc + h * 128
                v = VOLT[g, :, off:off + 128]
                lanes = pl.ds(pl.multiple_of(g * gf + off, 128), 128)
                st = states[:, lanes]
                opening = PB[0] * jnp.exp(PB[1] * v)
                closing = PB[2] * jnp.exp(-(PB[3] * v))
                total = opening + closing
                steady = opening / total
                fresh = steady + (st - steady) * jnp.exp(-time_step * total)
                live = (lane1 + h * 128) < cnt
                out_states[:, lanes] = jnp.where(live, fresh, st)
                cur = jnp.sum(tc * fresh * (v - PB[4]), axis=0, keepdims=True)
                out_cur[g, :, off:off + 128] = cur
        return carry

    lax.fori_loop(0, groups, ionic, 0)

    for dv, dm, other_m, ok in peers:
        guarded(ok, lambda a=dv, b=dm, o=other_m: cv_wait(a, b, o))

    nb = 3 * n_mem
    band = jnp.concatenate([CV[i, 0:1, :] for i in range(nb)] + [jnp.zeros((-nb % 16, 128), F32)], axis=0)
    hi, mid = split2(band)
    rest = (band - hi.astype(F32) - mid.astype(F32)).astype(BF16)
    lhs = jnp.concatenate([hi, mid, rest], axis=0)
    nbr = nb + (-nb % 16)
    gap = jnp.zeros((1, cells), F32)
    for j in range(partner.shape[0]):
        pos = partner[j:j + 1, :]
        slot_row = pos // cells - (me_v - 1) * n_mem
        col = pos % cells
        table = jnp.where(lax.broadcasted_iota(jnp.int32, (128, cells), 0) == col, 1.0, 0.0).astype(BF16)
        got = jnp.dot(lhs, table, preferred_element_type=F32)
        got = got[:nbr] + got[nbr:2 * nbr] + got[2 * nbr:]
        mask = lax.broadcasted_iota(jnp.int32, (nbr, cells), 0) == slot_row
        pv = jnp.sum(jnp.where(mask, got, 0.0), axis=0, keepdims=True)
        gap = gap + gcond[j:j + 1, :] * (cell_volt[:, :cells] - pv)

    def finish(g, carry):
        cur = []
        for q in range(gcells):
            c = g * gcells + q
            cnt = counts[c]
            share = jnp.sum(jnp.where(lane1[:, :cells] == c, gap, 0.0), axis=1, keepdims=True)
            share = share / jnp.maximum(jnp.full((1, fpc), cnt, jnp.int32), 1).astype(F32)
            ion = out_cur[g, :, q * fpc:(q + 1) * fpc]
            cur.append(jnp.where(slot_k < cnt, ion + share, 0.0))
        cur = jnp.concatenate(cur, axis=1)
        out_cur[g] = cur
        CUR[0, g] = cur
        return carry

    lax.fori_loop(0, groups, finish, 0)
    if trades:
        @pl.when(away)
        def _():
            table_far(2).start()
    bulk_start(2)
    for e in (0, 1):
        bulk_wait(e, order[:2])
        for ch in range(len(spans)):
            send_x(e, ch)
    if trades:
        @pl.when(away)
        def _():
            for k in range(3):
                table_far(k).wait_recv()

    def scatter(g, carry):
        cur = CUR[sel, g]
        hi = cur.astype(BF16).astype(F32)
        lo = cur - hi
        source = None
        for i, ref in enumerate((IN, EX)):
            idx = ref[sel, g]
            lane = idx & 127
            hot = lax.broadcasted_iota(jnp.int32, (128, gf), 0) == lane
            table = jnp.where(hot, 1.0, 0.0).astype(BF16)
            row = ((idx >> 7) & (zts - 1)) * 8 + ((idx // CZ) & 7)
            mask = lax.broadcasted_iota(jnp.int32, (8 * zts, gf), 0) == row
            sign = 1.0 if i == 0 else -1.0
            vals = jnp.concatenate(
                [jnp.where(mask, sign * part, 0.0).astype(BF16) for part in (hi, lo)], axis=0
            )
            put = lax.dot_general(vals, table, (((1,), (1,)), ((), ())), preferred_element_type=F32)
            source = put if source is None else source + put
        half = source.shape[0] // 2
        source = source[:half] + source[half:]
        gx, gy = g // ybs, g % ybs
        rows = pl.ds(pl.multiple_of(gy * 8, 8), 8)
        for z in range(zts):
            R[gx, rows, z * 128:(z + 1) * 128] = source[z * 8:(z + 1) * 8, :]
        return carry

    lax.fori_loop(0, groups, scatter, 0)

    for e in (0, 1):
        bulk_wait(e, order[2:])

    def put_y(dst, e):
        for p in range(CX):
            dst[p, 7:8, :] = YR[e, 0, p:p + 1, :]
            dst[p, 8 + CY:9 + CY, :] = YR[e, 1, p:p + 1, :]

    wait_y(0)
    put_y(C, 0)
    for ch in range(len(spans)):
        wait_x(0, ch)
    lane = lax.broadcasted_iota(jnp.int32, (8, CZ), 1)
    sub = lax.broadcasted_iota(jnp.int32, (8, CZ), 0)

    def views(src, halo, p, yb):
        base = pl.multiple_of(yb * 8, 8)
        rows = pl.ds(base + 8, 8)
        own = pl.ds(base, 8)
        centre = src[p, rows, :]
        below = halo[0, own, :] if p == 0 else src[p - 1, rows, :]
        above = halo[1, own, :] if p == CX - 1 else src[p + 1, rows, :]
        before = src[p, pl.ds(base, 8), :]
        after = src[p, pl.ds(pl.multiple_of(base + 16, 8), 8), :]
        return own, centre, (
            below, above,
            pltpu.roll(jnp.where(sub == 7, before, centre), 1, 0),
            pltpu.roll(jnp.where(sub == 0, after, centre), 7, 0),
            pltpu.roll(centre, 1, 1), pltpu.roll(centre, CZ - 1, 1),
        )

    def coeffs(yb, carry):
        for p in range(CX):
            own, centre, near = views(C, HX.at[0], p, yb)
            near = list(near)
            near[4] = jnp.where(lane == 0, 0.0, near[4])
            near[5] = jnp.where(lane == CZ - 1, 0.0, near[5])
            faces = [centre + n for n in near]
            total = faces[0] + faces[1] + faces[2] + faces[3] + faces[4] + faces[5]
            inv = 1.0 / (mass_coef + (0.5 * time_step) * total)
            scale = (0.5 * time_step) * inv
            faces[4] = jnp.where(lane == 0, 0.0, faces[4])
            faces[5] = jnp.where(lane == CZ - 1, 0.0, faces[5])
            for k in range(6):
                K[k, p, own, :] = faces[k] * scale
            R[p, own, :] = (mass_coef * X[0, p, pl.ds(pl.multiple_of(yb * 8, 8) + 8, 8), :] - time_step * R[p, own, :]) * inv
        return carry

    lax.fori_loop(0, ybs, coeffs, 0)

    def back_start(planes, ch):
        def far():
            for p in planes:
                back_far(p, ch).start()

        def near():
            for p in planes:
                back_near(p, ch).start()
        either(far, near)

    weights = sweep_weights()
    for t in range(ITERS):
        e = t + 1
        last = t == ITERS - 1
        wa, wb = weights[t]
        if last:
            for side in (0, 1):
                for ch in range(len(spans)):
                    guarded(has[0][side], lambda s=side, ch=ch: x_copy(1, s, ch, face_of(1, s, ch)).wait_send())

        def tile(p, yb, t=t, e=e, last=last, wa=wa, wb=wb):
            own, centre, near = views(X.at[t], HX.at[e], p, yb)
            acc = R[p, own, :] - centre
            for k in range(6):
                acc = acc + K[k, p, own, :] * near[k]
            step = wb * acc
            if t > 0:
                step = step + wa * U[p, own, :]
            new = centre + step
            if not last:
                U[p, own, :] = step
            X[(t + 1) % ITERS, p, pl.ds(pl.multiple_of(yb * 8, 8) + 8, 8), :] = new

        def sweep(planes, ch, tile=tile):
            def at(yb, carry):
                for p in planes:
                    tile(p, yb)
                return carry
            start, size = spans[ch]
            if size == 8:
                at(start // 8, 0)
            else:
                lax.fori_loop(start // 8, (start + size) // 8, at, 0)

        middle, faces = range(1, CX - 1), order[:2]
        for ch in range(edges, len(spans)):
            sweep(middle, ch)
            if last:
                back_start(middle, ch)
        wait_y(e)
        put_y(X.at[t], e)
        for ch in range(edges):
            sweep(middle, ch)
            if last:
                back_start(middle, ch)
        for ch in range(len(spans)):
            wait_x(e, ch)
            sweep(faces, ch)
            if last:
                back_start(faces, ch)
            elif ch == edges - 1:
                for p in range(CX):
                    YS[e + 1, 0, p:p + 1, :] = X[t + 1, p, 8:9, :]
                    YS[e + 1, 1, p:p + 1, :] = X[t + 1, p, 7 + CY:8 + CY, :]
                send_y(e + 1)
                for k in range(edges):
                    send_x(e + 1, k)
            elif ch >= edges:
                send_x(e + 1, ch)

    for e in range(ITERS + 1):
        for side in (0, 1):
            for ch in range(len(spans) if e != 1 else 0):
                guarded(has[0][side], lambda e=e, s=side, ch=ch: x_copy(e, s, ch, face_of(e, s, ch)).wait_send())
            guarded(y_ok(e, side), lambda e=e, s=side: y_copy(e, s).wait_send())
    for dv, dm, other_m, ok in peers:
        guarded(ok, lambda a=dv, b=dm, o=other_m: cv_copy(a, b, o).wait_send())

    def drain_far():
        for e in (0, 1):
            for p in range(CX):
                bulk_far(e, p).wait_send()
        for k in range(3):
            table_far(k).wait_send()
        for p in range(CX):
            for ch in range(len(spans)):
                back_far(p, ch).wait()

    def drain_near():
        for p in range(CX):
            for ch in range(len(spans)):
                back_near(p, ch).wait()
    either(drain_far, drain_near)


def per_device(
    n_vol, n_mem,
    potential, conductivity, ion_states, rate_scale, rate_slope, type_cond, reversal,
    facet_counts, intra_voxel, extra_voxel, cell_type, gap_partner, gap_cond,
):
    CX, CY, CZ = potential.shape
    nstates, facets = ion_states.shape
    cells = facet_counts.shape[0]
    ntypes = type_cond.shape[0]
    groups = CX * CY // 8
    gf = facets // groups
    ncols = 5 + ntypes
    vmem = pl.BlockSpec(memory_space=pltpu.VMEM)
    ex = ITERS + 1
    spans = len(row_spans(CY))
    nb = 3 * n_mem
    args = (
        potential, conductivity, ion_states, rate_scale, rate_slope, type_cond, reversal[None, :],
        facet_counts, cell_type,
        intra_voxel.reshape(groups, 1, gf), extra_voxel.reshape(groups, 1, gf), gap_partner.T, gap_cond.T,
    )
    args = tuple(pltpu.with_memory_space_constraint(a, pltpu.HBM) for a in args)
    held = [
        (pltpu.SMEM if a.ndim == 1 else pltpu.VMEM)(a.shape, a.dtype)
        for i, a in enumerate(args) if i not in (1, 9, 10)
    ]
    out = pl.pallas_call(
        functools.partial(kernel, n_vol, n_mem, ntypes),
        out_shape=(
            jax.ShapeDtypeStruct(potential.shape, F32),
            jax.ShapeDtypeStruct(ion_states.shape, F32),
            jax.ShapeDtypeStruct((groups, 1, gf), F32),
        ),
        in_specs=[pl.BlockSpec(memory_space=pltpu.HBM)] * len(args),
        out_specs=(vmem, vmem, vmem),
        scratch_shapes=held + [
            pltpu.SemaphoreType.DMA((14,)),
            pltpu.VMEM((2, groups, 1, gf), jnp.int32),
            pltpu.VMEM((2, groups, 1, gf), jnp.int32),
            pltpu.VMEM((2, groups, 1, gf), F32),
            pltpu.VMEM((2, CX, 8, CZ), F32),
            pltpu.VMEM((ITERS, CX, CY + 16, CZ), F32),
            pltpu.VMEM((CX, CY + 16, CZ), F32),
            pltpu.VMEM((6, CX, CY, CZ), F32),
            pltpu.VMEM((CX, CY, CZ), F32),
            pltpu.VMEM((CX, CY, CZ), F32),
            pltpu.VMEM((ex, 2, CY, CZ), F32),
            pltpu.VMEM((ex, 2, 8, CZ), F32),
            pltpu.VMEM((ex, 2, 8, CZ), F32),
            pltpu.VMEM((ncols, nstates, 128), F32),
            pltpu.VMEM((groups, 1, gf), F32),
            pltpu.VMEM((8, 128), F32),
            pltpu.VMEM((nb, 8, 128), F32),
            pltpu.SemaphoreType.DMA((ex, 2, spans)),
            pltpu.SemaphoreType.DMA((ex, 2, spans)),
            pltpu.SemaphoreType.DMA((ex, 2)),
            pltpu.SemaphoreType.DMA((ex, 2)),
            pltpu.SemaphoreType.DMA((nb,)),
            pltpu.SemaphoreType.DMA((nb,)),
            pltpu.SemaphoreType.DMA((2, CX)),
            pltpu.SemaphoreType.DMA((2, CX)),
            pltpu.SemaphoreType.DMA((3,)),
            pltpu.SemaphoreType.DMA((3,)),
            pltpu.SemaphoreType.DMA((CX, spans)),
            pltpu.SemaphoreType.DMA((CX, spans)),
        ],
        compiler_params=pltpu.CompilerParams(
            collective_id=0, has_side_effects=True, vmem_limit_bytes=42 * 1024 * 1024
        ),
    )(*args)
    return out[0], out[1], out[2].reshape(-1)


def solution(mesh):
    sizes = dict(mesh.shape)
    in_specs = (
        P("vol", "mem", None),
        P("vol", "mem", None),
        P(None, ("vol", "mem")),
        P(),
        P(),
        P(),
        P(),
        P(("vol", "mem")),
        P(("vol", "mem")),
        P(("vol", "mem")),
        P(("vol", "mem")),
        P(("vol", "mem"), None),
        P(("vol", "mem"), None),
    )
    out_specs = (P("vol", "mem", None), P(None, ("vol", "mem")), P(("vol", "mem")))
    return jax.shard_map(
        functools.partial(per_device, sizes["vol"], sizes["mem"]),
        mesh=mesh, in_specs=in_specs, out_specs=out_specs, check_vma=False,
    )
```
